32 devices in a mesh: chan: 4 (over z), win: 4 (over y, x), band: 2 (over core).
Axes of the slice: x: 2, y: 2, z: 4, core: 2. Of those that a mesh axis runs over, the one named last changes fastest.
Arguments:
- traces: bfloat16 [8, 1024, 4096], P('win', 'chan'), may hold values from -6 to 6
- send_rows: int32 [4, 4, 16], P('chan'), may hold values from 0 to 255
- pair_source: int32 [4096], P('chan'), may hold values from 0 to 255
- pair_slot: int32 [4096], P('chan'), may hold values from 0 to 63
- pair_owner: int32 [4096, 1], P('chan'), may hold values from 0 to 3; in each aligned block of 1024 rows (0 to 1023, 1024 to 2047, ...) at most 512 rows name the same one
- pair_bin: int32 [4096], P('chan'), may hold values from 0 to 15
Outputs:
- stacks: float32 [64, 512], P(('chan', 'win', 'band'))
The draws below stay inside these ranges and needn't reach their ends.
Inputs may be any that keep to these rules, and one draw needn't show every extreme that they name: `pair_owner`: in the pairs of one channel block no owner appears more than 512 times, and some owner appears exactly 512 times.
All inputs are finite; a program needn't handle non-finite values.
Results may differ from the reference program's by a relative error of at most 0.0049.
Values may be sent and summed in bfloat16 or wider, within the bound.
A program may use at most 64 MiB of HBM per device.

```python
import math
import jax
import jax.numpy as jnp
import numpy as np
from jax import lax

NS = 4096
NF = 1024
GROUP = 32
CB = 256
PAIRS_DEV = 1024
SLOTS = 16
BINS = 16
LAGS = 512
FLO = 128
BLOCKS = 4
CHANNELS = 1024
WIN = 8
TOTAL_PAIRS = 4096
STACKS = 64
CAP = 512


def set_ends(result, key, least, largest):
    spot = [jax.random.randint(jax.random.fold_in(key, axis), (), 0, length) for axis, length in enumerate(result.shape)]
    widest = result.shape.index(max(result.shape))
    beside = spot[:widest] + [(spot[widest] + 1) % result.shape[widest]] + spot[widest + 1:]
    return result.at[tuple(spot)].set(least).at[tuple(beside)].set(largest)


def level_of(key, shape, split, least, largest):
    level = 1.0
    for dim, shards_of in split:
        steps = jax.random.uniform(jax.random.fold_in(jax.random.fold_in(key, 6), dim), (shards_of,), jnp.float32, least / len(split), largest / len(split))
        level = level * jnp.repeat(jnp.exp(steps), shape[dim] // shards_of).reshape((-1,) + (1,) * (len(shape) - 1 - dim))
    return level


def shared_out(rng, own, number, rows, count, top, limit, lean):
    sequence = jax.random.permutation(rng, count)
    packed, usual = shares(count, rows * top, limit, lean, True), shares(count, rows * top, limit, lean, False)
    places = jnp.arange(count)

    def named(lengths, turn):
        used = int((lengths > 0).sum())
        fixed = max(1, used // 4)
        shifted = fixed + (places - fixed + turn * (used - fixed)) % max(1, count - fixed)
        return jnp.zeros((count,), jnp.int32).at[sequence[jnp.where(places < fixed, places, shifted)]].set(jnp.asarray(lengths, jnp.int32))

    lengths = jnp.where(number % 4 == 0, named(packed, number // 4), named(usual, number - number // 4 - 1))
    mixed = jax.random.permutation(jax.random.fold_in(own, 3), count)
    source_of, sink = mixed[0:count // 2 * 2:2], mixed[1:count // 2 * 2:2]
    slack = jnp.minimum(lengths[source_of] - 1, limit - lengths[sink]) // 2
    slack = jnp.where((source_of == sequence[0]) | (sink == sequence[0]) | (lengths[sink] == 0), 0, jnp.maximum(slack, 0))
    shifted = jax.random.randint(jax.random.fold_in(own, 4), (count // 2,), 0, 1 << 20) % (slack + 1)
    lengths = lengths.at[source_of].add(-shifted).at[sink].add(shifted)
    labels = jnp.searchsorted(jnp.cumsum(lengths), jnp.arange(rows * top), side="right").astype(jnp.int32)
    table = labels.reshape(top, rows).T
    table = table[jax.random.permutation(jax.random.fold_in(own, 1), rows)]
    turn = jax.random.randint(jax.random.fold_in(own, 2), (rows, 1), 0, top)
    return jnp.take_along_axis(table, (jnp.arange(top)[None, :] + turn) % top, axis=1)


def shares(number_of, total, limit, lean, full):
    portions = [(1 << 20) // math.isqrt(standing ** lean) + 1 for standing in range(1, number_of + 1)]
    largest = limit if full else min(limit, max(-(-total // number_of), total * portions[0] // sum(portions)))
    least = 1 if total - largest >= number_of - 1 else 0
    given, surplus = [largest] + [least] * (number_of - 1), total - largest - least * (number_of - 1)
    while surplus > 0:
        movable = [i for i in range(1, number_of) if given[i] < largest] or [i for i in range(1, number_of) if given[i] < limit]
        mass, left = sum([portions[i] for i in movable]), surplus
        for i in movable:
            extra = min(limit - given[i], max(1, left * portions[i] // mass), surplus)
            given[i] = given[i] + extra
            surplus = surplus - extra
    return np.array(given)


def bell_draw(key, dims, width, bound, split=(), kind=jnp.bfloat16):
    gain = level_of(key, dims, split, -0.22, 0.18) if split else 1.0
    array = jax.random.normal(key, dims, jnp.float32) * width * gain
    return jnp.minimum(jnp.maximum(array, -bound), bound).astype(kind)


def setup_inputs(seed: int = 0) -> dict:
    arg_keys = jax.random.split(jax.random.key(seed), 7)
    traces = bell_draw(arg_keys[0], (WIN, CHANNELS, NS), 1.0, 6.0, ((0, 4), (1, 4)))
    send_rows = set_ends(jax.random.randint(arg_keys[1], (BLOCKS, BLOCKS, SLOTS), 0, CB), jax.random.fold_in(arg_keys[1], 1), 0, CB - 1).astype(jnp.int32)
    pair_source = set_ends(jax.random.randint(arg_keys[2], (TOTAL_PAIRS,), 0, CB), jax.random.fold_in(arg_keys[2], 1), 0, CB - 1).astype(jnp.int32)
    pair_slot = set_ends(jax.random.randint(arg_keys[3], (TOTAL_PAIRS,), 0, BLOCKS * SLOTS), jax.random.fold_in(arg_keys[3], 1), 0, (BLOCKS * SLOTS) - 1).astype(jnp.int32)
    pair_owner_keys = jax.random.split(jax.random.fold_in(arg_keys[4], 1), TOTAL_PAIRS // PAIRS_DEV)
    pair_owner_turns = jax.random.permutation(jax.random.fold_in(arg_keys[4], 3), TOTAL_PAIRS // PAIRS_DEV)
    pair_owner = jax.vmap(lambda own, number: shared_out(jax.random.fold_in(arg_keys[4], 2), own, number, PAIRS_DEV, BLOCKS, 1, CAP, 2))(pair_owner_keys, pair_owner_turns).reshape((TOTAL_PAIRS, 1))
    pair_bin = set_ends(jax.random.randint(arg_keys[5], (TOTAL_PAIRS,), 0, BINS), jax.random.fold_in(arg_keys[5], 1), 0, BINS - 1).astype(jnp.int32)
    return dict(traces=traces, send_rows=send_rows, pair_source=pair_source, pair_slot=pair_slot, pair_owner=pair_owner, pair_bin=pair_bin)


def spectral_tables(first_bin, bin_count):
    sample_index = jnp.arange(NS, dtype=jnp.int32)[:, None]
    frequency = first_bin + jnp.arange(bin_count, dtype=jnp.int32)[None, :]
    phase_index = sample_index * frequency % NS
    angles = phase_index.astype(jnp.float32) * (2.0 * math.pi / NS)
    return (jnp.cos(angles).astype(jnp.bfloat16), (-jnp.sin(angles)).astype(jnp.bfloat16))

def whiten(real_part, imag_part):
    power_sum = real_part * real_part + imag_part * imag_part
    grouped = power_sum.reshape(power_sum.shape[:-1] + (power_sum.shape[-1] // GROUP, GROUP))
    power_mean = lax.optimization_barrier(jnp.mean(grouped, axis=-1))
    whiten_gain = jnp.repeat(lax.rsqrt(power_mean + 1e-05), GROUP, axis=-1)
    return ((real_part * whiten_gain).astype(jnp.bfloat16), (imag_part * whiten_gain).astype(jnp.bfloat16))

def reference(traces, send_rows, pair_source, pair_slot, pair_owner, pair_bin):
    cos_table, sin_table = spectral_tables(FLO, NF)

    def one_window(frame):
        spec_re = jnp.dot(frame, cos_table, preferred_element_type=jnp.float32)
        spec_im = jnp.dot(frame, sin_table, preferred_element_type=jnp.float32)
        white_re, white_im = whiten(spec_re, spec_im)
        return jnp.stack([white_re, white_im])
    whitened = lax.map(one_window, traces)
    pair_block = (jnp.arange(TOTAL_PAIRS, dtype=jnp.int32) // PAIRS_DEV).astype(jnp.int32)
    recv_block = (pair_slot // SLOTS).astype(jnp.int32)
    recv_entry = (pair_slot % SLOTS).astype(jnp.int32)
    receiver = recv_block * CB + send_rows[recv_block, pair_block, recv_entry]
    source = pair_block * CB + pair_source

    def accumulate(carry, frame):
        cross_re, cross_im = carry
        source_re = frame[0][source].astype(jnp.float32)
        source_im = frame[1][source].astype(jnp.float32)
        recv_re = frame[0][receiver].astype(jnp.float32)
        recv_im = frame[1][receiver].astype(jnp.float32)
        cross_re = cross_re + (source_re * recv_re + source_im * recv_im)
        cross_im = cross_im + (source_im * recv_re - source_re * recv_im)
        return ((cross_re, cross_im), None)
    start = (jnp.zeros((TOTAL_PAIRS, NF), jnp.float32), jnp.zeros((TOTAL_PAIRS, NF), jnp.float32))
    (cross_re, cross_im), _ = lax.scan(accumulate, start, whitened)
    stack_keys = pair_owner[:, 0] * BINS + pair_bin
    stack_re = jax.ops.segment_sum(cross_re, stack_keys, num_segments=STACKS)
    stack_im = jax.ops.segment_sum(cross_im, stack_keys, num_segments=STACKS)
    lag_index = jnp.arange(LAGS, dtype=jnp.int32) - LAGS // 2
    frequency = FLO + jnp.arange(NF, dtype=jnp.int32)
    phase_index = frequency[:, None] * (lag_index % NS)[None, :] % NS
    angles = phase_index.astype(jnp.float32) * (2.0 * math.pi / NS)
    cos_lag = jnp.cos(angles)
    sin_lag = jnp.sin(angles)
    scale = 1.0 / math.sqrt(WIN * NF * PAIRS_DEV / BINS)
    lagged = jnp.dot(stack_re, cos_lag, precision=lax.Precision.HIGHEST) - jnp.dot(stack_im, sin_lag, precision=lax.Precision.HIGHEST)
    return lagged * scale
```

```python
import functools
import math

import jax
import jax.numpy as jnp
import ml_dtypes
import numpy as np
from jax import lax
from jax.experimental import pallas as pl
from jax.experimental.pallas import tpu as pltpu
from jax.sharding import PartitionSpec as P

NS = 4096
NF = 1024
GROUP = 32
PAIRS_DEV = 1024
BINS = 16
LAGS = 512
FLO = 128
FB = 128
HALF = NS // 2
KC = 2048
KX = 512
BF = jnp.bfloat16
F32 = jnp.float32


def dot(a, b):
    return jnp.dot(a, b, preferred_element_type=F32)


def constants():
    angle = np.arange(NS, dtype=np.float64) * (2.0 * math.pi / NS)
    wave = np.stack([np.cos(angle), -np.sin(angle)]).astype(np.float32)
    freq = (FLO + np.arange(NF, dtype=np.int64)).reshape(NF // FB, 1, FB)
    fine = np.arange(FB, dtype=np.int64)[None, :, None] * freq % NS
    coarse = np.arange(0, HALF, FB, dtype=np.int64)[None, :, None] * freq % NS
    lag = ((np.arange(LAGS, dtype=np.int64) - LAGS // 2) % NS)[None, :]
    near = np.arange(FB, dtype=np.int64)[:, None] * lag % NS
    base = freq[:, 0, :1] * lag % NS
    swap = lambda t: np.ascontiguousarray(np.swapaxes(wave[:, t], 0, 1))
    return swap(fine), swap(coarse), wave[:, near], swap(base)


def turn(ca, sa, cb, sb):
    return ca * cb - sa * sb, sa * cb + ca * sb


def split(value):
    high = value.astype(BF)
    return high, (value - high.astype(F32)).astype(BF)


def columns(row, width):
    count = row.shape[1]
    spread = jnp.transpose(jnp.broadcast_to(row.astype(F32), (128, count)))
    parts = []
    for first in range(0, width, 128):
        lane = lax.broadcasted_iota(jnp.int32, (count, 128), 1).astype(F32) + float(first)
        parts.append(jnp.where(spread == lane, 1.0, 0.0).astype(BF))
    whole = parts[0] if len(parts) == 1 else jnp.concatenate(parts, axis=1)
    return whole[:, :width]


def kernel(
    send_ref, source_ref, slot_ref, owner_ref, bin_ref, x_hbm, fine_hbm, coarse_hbm, near_hbm, base_hbm, out_ref,
    x_ref, fine_ref, coarse_ref, near_ref, base_ref, hot_ref, sh_ref, rh_ref, kh_ref,
    white_ref, going_ref, recv_ref, lag_ref, part_ref, exch_ref,
    x_sem, table_sem, own_sem, send_sem, recv_sem, put_sem, get_sem, *, sizes, scale,
):
    blocks, windows, bands = sizes
    count = blocks * windows * bands
    chan, win, band = lax.axis_index("chan"), lax.axis_index("win"), lax.axis_index("band")
    me = (chan * windows + win) * bands + band
    nb, wins, chans = white_ref.shape[:3]
    slots, slot_count = hot_ref.shape[0], going_ref.shape[3]
    mesh_id = pl.DeviceIdType.MESH
    chunks = HALF // KX

    loads = [
        pltpu.make_async_copy(fine_hbm.at[pl.ds(band * nb, nb)], fine_ref, table_sem.at[0]),
        pltpu.make_async_copy(coarse_hbm.at[pl.ds(band * nb, nb)], coarse_ref, table_sem.at[1]),
    ]
    later = [
        pltpu.make_async_copy(near_hbm, near_ref, table_sem.at[2]),
        pltpu.make_async_copy(base_hbm.at[pl.ds(band * nb, nb)], base_ref, table_sem.at[3]),
    ]
    for k in range(2 * chunks):
        part = pl.ds(k * KX, KX)
        loads.append(pltpu.make_async_copy(x_hbm.at[:, part], x_ref.at[:, part], x_sem.at[k]))
    for load in loads + later:
        load.start()

    barrier = pltpu.get_barrier_semaphore()
    wins_at = [(win + d) % windows for d in range(windows)]
    bands_at = [(band + d) % bands for d in range(bands)]

    def peers(step):
        def group(dc, first):
            oc = (chan + dc) % blocks
            for dw in range(windows):
                for db in range(bands):
                    if not (first and dw == 0 and db == 0):
                        step((dc * windows + dw) * bands + db, (oc, wins_at[dw], bands_at[db]))

        def rest(dc, carry):
            group(dc, False)
            return carry

        lax.fori_loop(1, blocks, rest, 0)
        group(0, True)

    peers(lambda off, place: pl.semaphore_signal(barrier, inc=1, device_id=place, device_id_type=mesh_id))

    pick = lax.broadcasted_iota(jnp.int32, (slots, blocks), 0) // slot_count
    pick = jnp.where(pick == lax.broadcasted_iota(jnp.int32, (slots, blocks), 1), 1.0, 0.0).astype(BF)
    listed = dot(pick, send_ref[0].astype(F32).astype(BF))
    mine = lax.broadcasted_iota(jnp.int32, listed.shape, 0) % slot_count
    mine = mine == lax.broadcasted_iota(jnp.int32, listed.shape, 1)
    listed = jnp.sum(jnp.where(mine, listed, 0.0), axis=1, keepdims=True)
    lane = lax.broadcasted_iota(jnp.int32, hot_ref.shape, 1).astype(F32)
    hot_ref[...] = jnp.where(listed == lane, 1.0, 0.0).astype(BF)
    sh_ref[...] = columns(source_ref[...], sh_ref.shape[1])
    rh_ref[...] = columns(slot_ref[...], slots)
    row = lax.broadcasted_iota(jnp.int32, kh_ref.shape, 0)
    share = kh_ref.shape[0] // count
    key = owner_ref[...] * BINS + bin_ref[...]
    kh_ref[...] = jnp.where(row % count * share + row // count == key, 1.0, 0.0).astype(BF)
    lag_ref[...] = jnp.zeros_like(lag_ref)

    loads[0].wait()
    loads[1].wait()

    def sending(off, i):
        other = (chan + off) % blocks
        return pltpu.make_async_remote_copy(
            src_ref=going_ref.at[other, i], dst_ref=recv_ref.at[chan, i],
            send_sem=send_sem.at[off, i], recv_sem=recv_sem.at[off, i],
            device_id=(other, win, band), device_id_type=mesh_id,
        )

    def arriving(off, i):
        other = (chan - off + blocks) % blocks
        return pltpu.make_async_remote_copy(
            src_ref=going_ref.at[other, i], dst_ref=recv_ref.at[other, i],
            send_sem=send_sem.at[off, i], recv_sem=recv_sem.at[off, i],
            device_id=(other, win, band), device_id_type=mesh_id,
        )

    def staying(i):
        return pltpu.make_async_copy(going_ref.at[chan, i], recv_ref.at[chan, i], own_sem.at[i])

    lane = lax.broadcasted_iota(jnp.int32, (1, 2 * FB), 1)
    sign = (1 - 2 * (lane % 2)).astype(F32)
    a = lax.broadcasted_iota(jnp.int32, (FB, FB), 0) // GROUP
    b = lax.broadcasted_iota(jnp.int32, (FB, FB), 1) // GROUP
    ones = jnp.where(a == b, 1.0 / GROUP, 0.0).astype(BF)

    def transform(i, carry):
        even = odd = None
        for c in range(HALF // KC):
            parts = []
            for r in range(c * (KC // FB), (c + 1) * (KC // FB)):
                cos, sin = turn(fine_ref[i, 0], fine_ref[i, 1], coarse_ref[i, 0, r:r + 1], coarse_ref[i, 1, r:r + 1])
                parts.append(jnp.concatenate([cos.astype(BF), sin.astype(BF)], axis=1))
            table = jnp.concatenate(parts, axis=0)

            if i == 0:
                for k in range(c * KC // KX, (c + 1) * KC // KX):
                    loads[2 + k].wait()
                    loads[2 + chunks + k].wait()

            e = dot(x_ref[:, c * KC:(c + 1) * KC], table)
            o = dot(x_ref[:, HALF + c * KC:HALF + (c + 1) * KC], table)
            even, odd = (e, o) if even is None else (even + e, odd + o)
        spec = even + odd * sign
        re, im = spec[:, :FB], spec[:, FB:]
        high, low = split(re * re + im * im)
        gain = lax.rsqrt(dot(high, ones) + dot(low, ones) + 1e-05)
        white = jnp.concatenate([(re * gain).astype(BF), (im * gain).astype(BF)], axis=1)
        for w in range(wins):
            part = white[w * chans:(w + 1) * chans]
            white_ref[i, w] = part
            going_ref[:, i, w] = dot(hot_ref[...], part).astype(BF).reshape(blocks, slot_count, 2 * FB)

        if i == 0:
            pl.semaphore_wait(barrier, count - 1)

        def send(off, carry):
            sending(off, i).start()
            return carry

        if blocks <= 8:
            for off in range(1, blocks):
                send(off, 0)
        else:
            lax.fori_loop(1, blocks, send, 0)
        staying(i).start()
        return carry

    for i in range(nb):
        transform(i, 0)
    for load in later:
        load.wait()

    def stack(i, carry):
        def settle(off, carry):
            arriving(off, i).wait_recv()
            return carry

        base = base_ref[i]
        lh, ll = split(jnp.concatenate(turn(near_ref[0], near_ref[1], base[0:1], base[1:2]), axis=0))
        staying(i).wait()
        if blocks <= 8:
            for off in range(1, blocks):
                settle(off, 0)
        else:
            lax.fori_loop(1, blocks, settle, 0)
        cre = cim = None
        for w in range(wins):
            s = dot(sh_ref[...], white_ref[i, w])
            r = dot(rh_ref[...], recv_ref[:, i, w].reshape(slots, 2 * FB))
            sre, sim, rre, rim = s[:, :FB], s[:, FB:], r[:, :FB], r[:, FB:]
            tre, tim = sre * rre + sim * rim, sim * rre - sre * rim
            cre, cim = (tre, tim) if cre is None else (cre + tre, cim + tim)
        total = dot(kh_ref[...], jnp.concatenate([cre, cim], axis=1).astype(BF))
        th, tl = split(total)
        lag_ref[...] += dot(th, lh) + dot(tl, lh) + dot(th, ll)
        return carry

    for i in range(nb):
        stack(i, 0)
    pieces = LAGS // 128
    for j in range(share):
        for c in range(pieces):
            part_ref[:, j * pieces + c, :] = lag_ref[j * count:(j + 1) * count, c * 128:(c + 1) * 128]

    def putting(off, place):
        other = (place[0] * windows + place[1]) * bands + place[2]
        return pltpu.make_async_remote_copy(
            src_ref=part_ref.at[other], dst_ref=exch_ref.at[off],
            send_sem=put_sem.at[off], recv_sem=get_sem.at[off],
            device_id=place, device_id_type=mesh_id,
        )

    peers(lambda off, place: putting(off, place).start())
    exch_ref[0] = part_ref[me]
    peers(lambda off, place: putting(off, place).wait_recv())
    total = jnp.sum(exch_ref[...], axis=0) * scale
    for j in range(share):
        for c in range(pieces):
            out_ref[j:j + 1, c * 128:(c + 1) * 128] = total[j * pieces + c:j * pieces + c + 1]
    peers(lambda off, place: putting(off, place).wait_send())

    def drain(n, carry):
        sending(n // nb + 1, n % nb).wait_send()
        return carry

    lax.fori_loop(0, (blocks - 1) * nb, drain, 0)


def body(traces, send_rows, pair_source, pair_slot, pair_owner, pair_bin, *, tables):
    sizes = tuple(lax.axis_size(name) for name in ("chan", "win", "band"))
    blocks, windows, bands = sizes
    count = math.prod(sizes)
    nb = NF // FB // bands
    wins, chans, _ = traces.shape
    slot_count = send_rows.shape[2]
    slots, stacks, pairs = blocks * slot_count, blocks * BINS, pair_source.shape[0]
    share = stacks // count
    tile = (count, share * LAGS // 128, 128)
    scale = 1.0 / math.sqrt(wins * windows * NF * PAIRS_DEV / BINS)
    dma, vmem, here = pltpu.SemaphoreType.DMA, pltpu.VMEM, pl.BlockSpec(memory_space=pltpu.VMEM)
    return pl.pallas_call(
        functools.partial(kernel, sizes=sizes, scale=scale),
        out_shape=jax.ShapeDtypeStruct((share, LAGS), F32),
        in_specs=[here] * 5 + [pl.BlockSpec(memory_space=pl.ANY)] * 5,
        out_specs=here,
        scratch_shapes=[
            vmem((wins * chans, NS), BF),
            vmem((nb, 2, FB, FB), F32),
            vmem((nb, 2, HALF // FB, FB), F32),
            vmem((2, FB, LAGS), F32),
            vmem((nb, 2, LAGS), F32),
            vmem((slots, chans), BF),
            vmem((pairs, chans), BF),
            vmem((pairs, slots), BF),
            vmem((stacks, pairs), BF),
            vmem((nb, wins, chans, 2 * FB), BF),
            vmem((blocks, nb, wins, slot_count, 2 * FB), BF),
            vmem((blocks, nb, wins, slot_count, 2 * FB), BF),
            vmem((stacks, LAGS), F32),
            vmem(tile, F32),
            vmem(tile, F32),
            dma((2 * HALF // KX,)), dma((4,)), dma((nb,)), dma((blocks, nb)), dma((blocks, nb)), dma((count,)), dma((count,)),
        ],
        compiler_params=pltpu.CompilerParams(vmem_limit_bytes=60 << 20, collective_id=0, has_side_effects=True),
    )(
        send_rows, pair_source.reshape(1, pairs), pair_slot.reshape(1, pairs), pair_owner.reshape(1, pairs),
        pair_bin.reshape(1, pairs), traces.reshape(wins * chans, NS), *tables,
    )


def solution(mesh):
    tables = constants()
    return jax.shard_map(
        functools.partial(body, tables=tables),
        mesh=mesh,
        in_specs=(
            P("win", "chan", None),
            P("chan", None, None),
            P("chan"),
            P("chan"),
            P("chan", None),
            P("chan"),
        ),
        out_specs=P(("chan", "win", "band"), None),
        check_vma=False,
    )
```

```python
import functools
import math

import jax
import jax.numpy as jnp
import numpy as np
from jax import lax
from jax.experimental import pallas as pl
from jax.experimental.pallas import tpu as pltpu
from jax.sharding import PartitionSpec as P

NS = 4096
NF = 1024
GROUP = 32
PAIRS_DEV = 1024
BINS = 16
LAGS = 512
FLO = 128
FB = 128
RADIX = 4
NQ = NS // RADIX
KX = 512
BF = jnp.bfloat16
F32 = jnp.float32


def dot(a, b):
    return jnp.dot(a, b, preferred_element_type=F32)


def constants():
    angle = np.arange(NS, dtype=np.float64) * (2.0 * math.pi / NS)
    wave = np.stack([np.cos(angle), -np.sin(angle)]).astype(np.float32)
    freq = (FLO + np.arange(NF, dtype=np.int64)).reshape(-1, FB, RADIX).swapaxes(1, 2).reshape(-1, 1, FB)
    steps = np.concatenate([np.arange(0, NQ, FB), np.arange(0, FB, 8), np.arange(8)]).astype(np.int64)
    steps = steps[None, :, None] * freq % NS
    lag = ((np.arange(LAGS, dtype=np.int64) - LAGS // 2) % NS)[None, :]
    swap = lambda t: np.ascontiguousarray(np.swapaxes(wave[:, t], 0, 1))
    turns = swap(freq.reshape(-1, FB, 1) * lag % NS).reshape(-1, 2 * FB, LAGS)
    high = turns.astype(BF)
    low = (turns - high.astype(np.float32)).astype(BF)
    return swap(steps), np.stack([high, low], axis=1)


def turn(ca, sa, cb, sb):
    return ca * cb - sa * sb, sa * cb + ca * sb


def split(value):
    high = value.astype(BF)
    return high, (value - high.astype(F32)).astype(BF)


def columns(row, width):
    count = row.shape[1]
    spread = jnp.transpose(jnp.broadcast_to(row.astype(F32), (128, count)))
    parts = []
    for first in range(0, width, 128):
        lane = lax.broadcasted_iota(jnp.int32, (count, 128), 1).astype(F32) + float(first)
        parts.append(jnp.where(spread == lane, 1.0, 0.0).astype(BF))
    whole = parts[0] if len(parts) == 1 else jnp.concatenate(parts, axis=1)
    return whole[:, :width]


def kernel(
    send_hbm, source_hbm, slot_hbm, owner_hbm, bin_hbm, x_hbm, steps_hbm, turns_hbm, out_ref,
    send_ref, source_ref, slot_ref, owner_ref, bin_ref, x_ref, steps_ref, turns_ref, table_ref, fold_ref, hot_ref, sh_ref, rh_ref, kh_ref,
    white_ref, src_ref, cross_ref, going_ref, recv_ref, lag_ref, part_ref, exch_ref,
    list_sem, x_sem, table_sem, send_sem, recv_sem, put_sem, get_sem, ready_sem, *, sizes, scale,
):
    blocks, windows, bands = sizes
    count = blocks * windows * bands
    chan, win, band = lax.axis_index("chan"), lax.axis_index("win"), lax.axis_index("band")
    me = (chan * windows + win) * bands + band
    wins, chans = white_ref.shape[0], white_ref.shape[2]
    slots, slot_count = hot_ref.shape[0], going_ref.shape[3]
    pairs = sh_ref.shape[0]
    mesh_id = pl.DeviceIdType.MESH
    chunks = NQ // KX

    mine = pl.ds(band * RADIX, RADIX)
    steps = pltpu.make_async_copy(steps_hbm.at[mine], steps_ref, table_sem.at[0])
    lists = [
        pltpu.make_async_copy(here, there, list_sem.at[n]) for n, (here, there) in enumerate((
            (send_hbm, send_ref), (source_hbm, source_ref), (slot_hbm, slot_ref), (owner_hbm, owner_ref), (bin_hbm, bin_ref),
        ))
    ]
    later = pltpu.make_async_copy(turns_hbm.at[mine], turns_ref, table_sem.at[1])
    frames = {}
    for w in range(wins):
        for q in range(chunks):
            for a in range(RADIX):
                rows, part = pl.ds(w * chans, chans), pl.ds(a * NQ + q * KX, KX)
                frames[w, q, a] = pltpu.make_async_copy(
                    x_hbm.at[rows, part], x_ref.at[rows, part], x_sem.at[(w * chunks + q) * RADIX + a]
                )
    def fetch(w):
        for q in range(chunks):
            for a in range(RADIX):
                frames[w, q, a].start()

    steps.start()
    for load in lists:
        load.start()
    fetch(0)

    barrier = pltpu.get_barrier_semaphore()

    def away(off, back=False):
        if blocks == 4:
            return {1: chan + 1 - 2 * (chan % 2), 2: (chan + 2) % 4, 3: 3 - chan}[off]
        return (chan - off + blocks) % blocks if back else (chan + off) % blocks

    def along(step):
        if blocks <= 8:
            for off in (2, 3, 1) if blocks == 4 else range(1, blocks):
                step(off)
        else:
            lax.fori_loop(1, blocks, lambda off, carry: (step(off), carry)[1], 0)

    plane = [
        (dw, db, (chan, (win + dw) % windows, (band + db) % bands))
        for dw in range(windows) for db in range(bands) if dw or db
    ]

    def hail(place, semaphore):
        pl.semaphore_signal(semaphore, inc=1, device_id=place, device_id_type=mesh_id)

    along(lambda off: hail((away(off), win, band), barrier))
    for _, _, place in plane:
        hail(place, barrier)

    for w in range(1, wins):
        fetch(w)

    steps.wait()
    for load in lists:
        load.wait()
    pick = lax.broadcasted_iota(jnp.int32, (slots, blocks), 0) // slot_count
    pick = jnp.where(pick == lax.broadcasted_iota(jnp.int32, (slots, blocks), 1), 1.0, 0.0).astype(BF)
    listed = dot(pick, send_ref[0].astype(F32).astype(BF))
    own = lax.broadcasted_iota(jnp.int32, listed.shape, 0) % slot_count
    own = own == lax.broadcasted_iota(jnp.int32, listed.shape, 1)
    listed = jnp.sum(jnp.where(own, listed, 0.0), axis=1, keepdims=True)
    lane = lax.broadcasted_iota(jnp.int32, hot_ref.shape, 1).astype(F32)
    hot_ref[...] = jnp.where(listed == lane, 1.0, 0.0).astype(BF)
    share = kh_ref.shape[0] // count
    a = lax.broadcasted_iota(jnp.int32, (2 * FB, FB), 0) % FB // (GROUP // RADIX)
    b = lax.broadcasted_iota(jnp.int32, (2 * FB, FB), 1) // (GROUP // RADIX)
    ones = jnp.where(a == b, 1.0 / GROUP, 0.0).astype(BF)

    def tables():
        tiny = steps_ref.shape[2] - 8
        for j in range(RADIX):
            wave = lambda r: (steps_ref[j, 0, r:r + 1], steps_ref[j, 1, r:r + 1])
            fine = [turn(steps_ref[j, 0, tiny:], steps_ref[j, 1, tiny:], *wave(r)) for r in range(NQ // FB, tiny)]
            fine = [jnp.concatenate(part, axis=0) for part in zip(*fine)]
            for r in range(NQ // FB):
                cos, sin = turn(*fine, *wave(r))
                table_ref[j, r * FB:(r + 1) * FB, :] = jnp.concatenate([cos.astype(BF), sin.astype(BF)], axis=1)

    def places():
        sh_ref[...] = columns(source_ref[...], sh_ref.shape[1])
        rh_ref[...] = columns(slot_ref[...], slots)
        row = lax.broadcasted_iota(jnp.int32, kh_ref.shape, 0)
        key = owner_ref[...] * BINS + bin_ref[...]
        kh_ref[...] = jnp.where(row % count * share + row // count == key, 1.0, 0.0).astype(BF)

    def spectra(ref, w):
        rows = ref.shape[2]
        ends = ref[w, 2:4].reshape(2 * rows, NQ)
        s0, s2 = dot(ref[w, 0], table_ref[0]), dot(ref[w, 1], table_ref[2])
        o1, o3 = dot(ends, table_ref[1]), dot(ends, table_ref[3])
        re = [s0[:, :FB], o1[:rows, :FB] + o1[rows:, FB:], s2[:, :FB], o3[:rows, :FB] - o3[rows:, FB:]]
        im = [s0[:, FB:], o1[:rows, FB:] - o1[rows:, :FB], s2[:, FB:], o3[:rows, FB:] + o3[rows:, :FB]]
        power = sum(u * u + v * v for u, v in zip(re, im))
        gain = lax.rsqrt(dot(jnp.concatenate(split(power), axis=1), ones) + 1e-05)
        return [jnp.concatenate([(u * gain).astype(BF), (v * gain).astype(BF)], axis=1) for u, v in zip(re, im)]

    def sending(off, w, h):
        other = away(off)
        part = pl.ds(2 * h, 2)
        return pltpu.make_async_remote_copy(
            src_ref=going_ref.at[other, w, part], dst_ref=recv_ref.at[chan, w, part],
            send_sem=send_sem.at[off, 2 * w + h], recv_sem=recv_sem.at[off, 2 * w + h],
            device_id=(other, win, band), device_id_type=mesh_id,
        )

    def arriving(off, w, h):
        other = away(off, True)
        part = pl.ds(2 * h, 2)
        return pltpu.make_async_remote_copy(
            src_ref=going_ref.at[other, w, part], dst_ref=recv_ref.at[other, w, part],
            send_sem=send_sem.at[off, 2 * w + h], recv_sem=recv_sem.at[off, 2 * w + h],
            device_id=(other, win, band), device_id_type=mesh_id,
        )

    for w in range(wins):
        rows = slice(w * chans, (w + 1) * chans)
        for q in range(chunks):
            for a in range(RADIX):
                frames[w, q, a].wait()
        if w == 0:
            tables()
        if w == wins - 1:
            places()
        for q in range(chunks):
            x0, x1, x2, x3 = (x_ref[rows, a * NQ + q * KX:a * NQ + (q + 1) * KX] for a in range(RADIX))
            ends = x0 - x2, x1 - x3
            even, odd = x0.astype(F32) + x2.astype(F32), x1.astype(F32) + x3.astype(F32)
            for kind, value in enumerate(((even + odd).astype(BF), (even - odd).astype(BF), *ends)):
                fold_ref[w, kind, :, q * KX:(q + 1) * KX] = value
        for j, part in enumerate(spectra(fold_ref, w)):
            white_ref[w, j] = part
            going_ref[:, w, j] = dot(hot_ref[...], part).astype(BF).reshape(blocks, slot_count, 2 * FB)
        if w == 0:
            later.start()
            pl.semaphore_wait(barrier, blocks - 1 + len(plane))
            along(lambda off: hail((away(off), win, band), ready_sem))
        for h in range(RADIX // 2):
            along(lambda off: sending(off, w, h).start())
        recv_ref[chan, w] = going_ref[chan, w]

    for w in range(wins):
        for j in range(RADIX):
            src_ref[w, j] = dot(sh_ref[...], white_ref[w, j])
    later.wait()
    lag = None
    for w in range(wins):
        for j in range(RADIX):
            if j % 2 == 0:
                along(lambda off: arriving(off, w, j // 2).wait_recv())
            s = src_ref[w, j]
            r = dot(rh_ref[...], recv_ref[:, w, j].reshape(slots, 2 * FB))
            sre, sim, rre, rim = s[:, :FB], s[:, FB:], r[:, :FB], r[:, FB:]
            total = jnp.concatenate([sre * rre + sim * rim, sim * rre - sre * rim], axis=1)
            if w:
                total = total + cross_ref[j]
            if w < wins - 1:
                cross_ref[j] = total
                continue
            high, low = split(dot(kh_ref[...], total.astype(BF)))
            both = dot(jnp.concatenate([high, low], axis=0), turns_ref[j, 0])
            term = both[:high.shape[0]] + both[high.shape[0]:] + dot(high, turns_ref[j, 1])
            lag = term if lag is None else lag + term
    lag_ref[...] = lag

    pieces = LAGS // 128
    for j in range(share):
        for c in range(pieces):
            part_ref[:, j * pieces + c, :] = lag_ref[j * count:(j + 1) * count, c * 128:(c + 1) * 128]

    def peers(step):
        def group(dc, first):
            oc = (chan + dc) % blocks if isinstance(dc, int) and dc == 0 else away(dc)
            for dw in range(windows):
                for db in range(bands):
                    if not (first and dw == 0 and db == 0):
                        step((dc * windows + dw) * bands + db, (oc, (win + dw) % windows, (band + db) % bands))

        along(lambda dc: group(dc, False))
        group(0, True)

    def putting(off, place):
        other = (place[0] * windows + place[1]) * bands + place[2]
        return pltpu.make_async_remote_copy(
            src_ref=part_ref.at[other], dst_ref=exch_ref.at[off],
            send_sem=put_sem.at[off], recv_sem=get_sem.at[off],
            device_id=place, device_id_type=mesh_id,
        )

    pl.semaphore_wait(ready_sem, blocks - 1)
    peers(lambda off, place: putting(off, place).start())
    exch_ref[0] = part_ref[me]
    peers(lambda off, place: putting(off, place).wait_recv())
    total = jnp.sum(exch_ref[...], axis=0) * scale
    for j in range(share):
        for c in range(pieces):
            out_ref[j:j + 1, c * 128:(c + 1) * 128] = total[j * pieces + c:j * pieces + c + 1]
    peers(lambda off, place: putting(off, place).wait_send())
    for w in range(wins):
        for h in range(RADIX // 2):
            along(lambda off: sending(off, w, h).wait_send())


def body(traces, send_rows, pair_source, pair_slot, pair_owner, pair_bin, *, tables):
    sizes = tuple(lax.axis_size(name) for name in ("chan", "win", "band"))
    blocks, windows, bands = sizes
    count = math.prod(sizes)
    wins, chans, _ = traces.shape
    slot_count = send_rows.shape[2]
    slots, stacks, pairs = blocks * slot_count, blocks * BINS, pair_source.shape[0]
    share = stacks // count
    tile = (count, share * LAGS // 128, 128)
    scale = 1.0 / math.sqrt(wins * windows * NF * PAIRS_DEV / BINS)
    dma, vmem, here = pltpu.SemaphoreType.DMA, pltpu.VMEM, pl.BlockSpec(memory_space=pltpu.VMEM)
    return pl.pallas_call(
        functools.partial(kernel, sizes=sizes, scale=scale),
        out_shape=jax.ShapeDtypeStruct((share, LAGS), F32),
        in_specs=[pl.BlockSpec(memory_space=pl.ANY)] * 8,
        out_specs=here,
        scratch_shapes=[
            vmem(send_rows.shape, jnp.int32),
            *[vmem((1, pairs), jnp.int32)] * 4,
            vmem((wins * chans, NS), BF),
            vmem((RADIX, *tables[0].shape[1:]), F32),
            vmem((RADIX, 2, 2 * FB, LAGS), BF),
            vmem((RADIX, NQ, 2 * FB), BF),
            vmem((wins, RADIX, chans, NQ), BF),
            vmem((slots, chans), BF),
            vmem((pairs, chans), BF),
            vmem((pairs, slots), BF),
            vmem((stacks, pairs), BF),
            vmem((wins, RADIX, chans, 2 * FB), BF),
            vmem((wins, RADIX, pairs, 2 * FB), F32),
            vmem((RADIX, pairs, 2 * FB), F32),
            vmem((blocks, wins, RADIX, slot_count, 2 * FB), BF),
            vmem((blocks, wins, RADIX, slot_count, 2 * FB), BF),
            vmem((stacks, LAGS), F32),
            vmem(tile, F32),
            vmem(tile, F32),
            dma((5,)), dma((wins * NS // KX,)), dma((2,)), dma((blocks, 2 * wins)), dma((blocks, 2 * wins)), dma((count,)), dma((count,)),
            pltpu.SemaphoreType.REGULAR,
        ],
        compiler_params=pltpu.CompilerParams(vmem_limit_bytes=60 << 20, collective_id=0, has_side_effects=True),
    )(
        send_rows, pair_source.reshape(1, pairs), pair_slot.reshape(1, pairs), pair_owner.reshape(1, pairs),
        pair_bin.reshape(1, pairs), traces.reshape(wins * chans, NS), *tables,
    )


def solution(mesh):
    tables = constants()
    return jax.shard_map(
        functools.partial(body, tables=tables),
        mesh=mesh,
        in_specs=(
            P("win", "chan", None),
            P("chan", None, None),
            P("chan"),
            P("chan"),
            P("chan", None),
            P("chan"),
        ),
        out_specs=P(("chan", "win", "band"), None),
        check_vma=False,
    )
```

```python
import functools
import math

import jax
import jax.numpy as jnp
import numpy as np
from jax import lax
from jax.experimental import pallas as pl
from jax.experimental.pallas import tpu as pltpu
from jax.sharding import PartitionSpec as P

NS = 4096
NF = 1024
GROUP = 32
PAIRS_DEV = 1024
BINS = 16
LAGS = 512
FLO = 128
FB = 128
RADIX = 4
NQ = NS // RADIX
KX = 512
BF = jnp.bfloat16
F32 = jnp.float32


def dot(a, b):
    return jnp.dot(a, b, preferred_element_type=F32)


def constants():
    angle = np.arange(NS, dtype=np.float64) * (2.0 * math.pi / NS)
    wave = np.stack([np.cos(angle), -np.sin(angle)]).astype(np.float32)
    freq = (FLO + np.arange(NF, dtype=np.int64)).reshape(-1, FB, RADIX).swapaxes(1, 2).reshape(-1, 1, FB)
    steps = np.arange(NQ, dtype=np.int64)[None, :, None] * freq % NS
    steps = np.concatenate([wave[0][steps], wave[1][steps]], axis=2).astype(BF)
    lag = ((np.arange(LAGS, dtype=np.int64) - LAGS // 2) % NS)[None, :]
    swap = lambda t: np.ascontiguousarray(np.swapaxes(wave[:, t], 0, 1))
    turns = swap(freq.reshape(-1, FB, 1) * lag % NS).reshape(-1, 2 * FB, LAGS)
    high = turns.astype(BF)
    low = (turns - high.astype(np.float32)).astype(BF)
    return steps, np.stack([high, low], axis=1)


def turn(ca, sa, cb, sb):
    return ca * cb - sa * sb, sa * cb + ca * sb


def split(value):
    high = value.astype(BF)
    return high, (value - high.astype(F32)).astype(BF)


def columns(row, width):
    count = row.shape[1]
    spread = jnp.transpose(jnp.broadcast_to(row.astype(F32), (128, count)))
    parts = []
    for first in range(0, width, 128):
        lane = lax.broadcasted_iota(jnp.int32, (count, 128), 1).astype(F32) + float(first)
        parts.append(jnp.where(spread == lane, 1.0, 0.0).astype(BF))
    whole = parts[0] if len(parts) == 1 else jnp.concatenate(parts, axis=1)
    return whole[:, :width]


def kernel(
    send_hbm, source_hbm, slot_hbm, owner_hbm, bin_hbm, x_hbm, steps_hbm, turns_hbm, out_ref,
    send_ref, source_ref, slot_ref, owner_ref, bin_ref, x_ref, turns_ref, table_ref, fold_ref, pick_ref, hot_ref, sh_ref, rh_ref, kh_ref,
    src_ref, cross_ref, going_ref, recv_ref, lag_ref, part_ref, exch_ref,
    list_sem, x_sem, table_sem, send_sem, recv_sem, put_sem, get_sem, ready_sem, *, sizes, scale,
):
    blocks, windows, bands = sizes
    count = blocks * windows * bands
    chan, win, band = lax.axis_index("chan"), lax.axis_index("win"), lax.axis_index("band")
    me = (chan * windows + win) * bands + band
    wins, chans = fold_ref.shape[0], fold_ref.shape[2]
    slots, slot_count = hot_ref.shape[0], going_ref.shape[3]
    pairs = sh_ref.shape[0]
    mesh_id = pl.DeviceIdType.MESH
    chunks = NQ // KX

    mine = pl.ds(band * RADIX, RADIX)
    steps = [
        pltpu.make_async_copy(steps_hbm.at[band * RADIX + j], table_ref.at[j], table_sem.at[2 + j]) for j in range(RADIX)
    ]
    lists = [
        pltpu.make_async_copy(here, there, list_sem.at[n]) for n, (here, there) in enumerate((
            (send_hbm, send_ref), (source_hbm, source_ref), (slot_hbm, slot_ref), (owner_hbm, owner_ref), (bin_hbm, bin_ref),
        ))
    ]
    later = pltpu.make_async_copy(turns_hbm.at[mine], turns_ref, table_sem.at[1])
    frames = {}
    for w in range(wins):
        for q in range(chunks):
            for a in range(RADIX):
                rows, part = pl.ds(w * chans, chans), pl.ds(a * NQ + q * KX, KX)
                frames[w, q, a] = pltpu.make_async_copy(
                    x_hbm.at[rows, part], x_ref.at[rows, part], x_sem.at[(w * chunks + q) * RADIX + a]
                )
    def fetch(w):
        for q in range(chunks):
            for a in range(RADIX):
                frames[w, q, a].start()

    for load in lists:
        load.start()
    fetch(0)
    for load in steps:
        load.start()

    barrier = pltpu.get_barrier_semaphore()

    def away(off, back=False):
        if blocks == 4:
            return {1: chan + 1 - 2 * (chan % 2), 2: (chan + 2) % 4, 3: 3 - chan}[off]
        return (chan - off + blocks) % blocks if back else (chan + off) % blocks

    def along(step):
        if blocks <= 8:
            for off in (2, 3, 1) if blocks == 4 else range(1, blocks):
                step(off)
        else:
            lax.fori_loop(1, blocks, lambda off, carry: (step(off), carry)[1], 0)

    plane = [
        (dw, db, (chan, (win + dw) % windows, (band + db) % bands))
        for dw in range(windows) for db in range(bands) if dw or db
    ]

    def hail(place, semaphore):
        pl.semaphore_signal(semaphore, inc=1, device_id=place, device_id_type=mesh_id)

    along(lambda off: hail((away(off), win, band), barrier))
    for _, _, place in plane:
        hail(place, barrier)


    for load in lists:
        load.wait()
    for w in range(1, wins):
        fetch(w)
    pick = lax.broadcasted_iota(jnp.int32, (slots, blocks), 0) // slot_count
    pick = jnp.where(pick == lax.broadcasted_iota(jnp.int32, (slots, blocks), 1), 1.0, 0.0).astype(BF)
    listed = dot(pick, send_ref[0].astype(F32).astype(BF))
    own = lax.broadcasted_iota(jnp.int32, listed.shape, 0) % slot_count
    own = own == lax.broadcasted_iota(jnp.int32, listed.shape, 1)
    listed = jnp.sum(jnp.where(own, listed, 0.0), axis=1, keepdims=True)
    lane = lax.broadcasted_iota(jnp.int32, hot_ref.shape, 1).astype(F32)
    hot_ref[...] = jnp.where(listed == lane, 1.0, 0.0).astype(BF)
    share = kh_ref.shape[0] // count
    a = lax.broadcasted_iota(jnp.int32, (2 * FB, FB), 0) % FB // (GROUP // RADIX)
    b = lax.broadcasted_iota(jnp.int32, (2 * FB, FB), 1) // (GROUP // RADIX)
    ones = jnp.where(a == b, 1.0 / GROUP, 0.0).astype(BF)

    def places():
        sh_ref[...] = columns(source_ref[...], sh_ref.shape[1])
        rh_ref[...] = columns(slot_ref[...], slots)
        row = lax.broadcasted_iota(jnp.int32, kh_ref.shape, 0)
        key = owner_ref[...] * BINS + bin_ref[...]
        kh_ref[...] = jnp.where(row % count * share + row // count == key, 1.0, 0.0).astype(BF)

    def spectra(ref, w):
        rows = ref.shape[2]
        ends = ref[w, 2:4].reshape(2 * rows, NQ)
        s0, s2 = dot(ref[w, 0], table_ref[0]), dot(ref[w, 1], table_ref[2])
        o1, o3 = dot(ends, table_ref[1]), dot(ends, table_ref[3])
        re = [s0[:, :FB], o1[:rows, :FB] + o1[rows:, FB:], s2[:, :FB], o3[:rows, :FB] - o3[rows:, FB:]]
        im = [s0[:, FB:], o1[:rows, FB:] - o1[rows:, :FB], s2[:, FB:], o3[:rows, FB:] + o3[rows:, :FB]]
        power = sum(u * u + v * v for u, v in zip(re, im))
        gain = lax.rsqrt(dot(jnp.concatenate(split(power), axis=1), ones) + 1e-05)
        return [jnp.concatenate([(u * gain).astype(BF), (v * gain).astype(BF)], axis=1) for u, v in zip(re, im)]

    def sending(off, w, h):
        other = away(off)
        part = pl.ds(2 * h, 2)
        return pltpu.make_async_remote_copy(
            src_ref=going_ref.at[other, w, part], dst_ref=recv_ref.at[chan, w, part],
            send_sem=send_sem.at[off, 2 * w + h], recv_sem=recv_sem.at[off, 2 * w + h],
            device_id=(other, win, band), device_id_type=mesh_id,
        )

    def arriving(off, w, h):
        other = away(off, True)
        part = pl.ds(2 * h, 2)
        return pltpu.make_async_remote_copy(
            src_ref=going_ref.at[other, w, part], dst_ref=recv_ref.at[other, w, part],
            send_sem=send_sem.at[off, 2 * w + h], recv_sem=recv_sem.at[off, 2 * w + h],
            device_id=(other, win, band), device_id_type=mesh_id,
        )

    for w in range(wins):
        rows = slice(w * chans, (w + 1) * chans)
        for q in range(chunks):
            for a in range(RADIX):
                frames[w, q, a].wait()
        if w == 0:
            for load in steps:
                load.wait()
        for q in range(chunks):
            x0, x1, x2, x3 = (x_ref[rows, a * NQ + q * KX:a * NQ + (q + 1) * KX] for a in range(RADIX))
            ends = x0 - x2, x1 - x3
            even, odd = x0.astype(F32) + x2.astype(F32), x1.astype(F32) + x3.astype(F32)
            for kind, value in enumerate(((even + odd).astype(BF), (even - odd).astype(BF), *ends)):
                fold_ref[w, kind, :, q * KX:(q + 1) * KX] = value
        for kind in range(RADIX):
            pick_ref[w, kind] = dot(hot_ref[...], fold_ref[w, kind]).astype(BF)
        for j, part in enumerate(spectra(pick_ref, w)):
            going_ref[:, w, j] = part.reshape(blocks, slot_count, 2 * FB)
        if w == 0:
            later.start()
            pl.semaphore_wait(barrier, blocks - 1 + len(plane))
            along(lambda off: hail((away(off), win, band), ready_sem))
        for h in range(RADIX // 2):
            along(lambda off: sending(off, w, h).start())
        recv_ref[chan, w] = going_ref[chan, w]

    places()
    for w in range(wins):
        for j, part in enumerate(spectra(fold_ref, w)):
            src_ref[w, j] = dot(sh_ref[...], part)
    later.wait()
    lag = None
    for w in range(wins):
        for j in range(RADIX):
            if j % 2 == 0:
                along(lambda off: arriving(off, w, j // 2).wait_recv())
            s = src_ref[w, j]
            r = dot(rh_ref[...], recv_ref[:, w, j].reshape(slots, 2 * FB))
            sre, sim, rre, rim = s[:, :FB], s[:, FB:], r[:, :FB], r[:, FB:]
            total = jnp.concatenate([sre * rre + sim * rim, sim * rre - sre * rim], axis=1)
            if w:
                total = total + cross_ref[j]
            if w < wins - 1:
                cross_ref[j] = total
                continue
            high, low = split(dot(kh_ref[...], total.astype(BF)))
            both = dot(jnp.concatenate([high, low], axis=0), turns_ref[j, 0])
            term = both[:high.shape[0]] + both[high.shape[0]:] + dot(high, turns_ref[j, 1])
            lag = term if lag is None else lag + term
    lag_ref[...] = lag

    pieces = LAGS // 128
    for j in range(share):
        for c in range(pieces):
            part_ref[:, j * pieces + c, :] = lag_ref[j * count:(j + 1) * count, c * 128:(c + 1) * 128]

    def peers(step):
        def group(dc, first):
            oc = (chan + dc) % blocks if isinstance(dc, int) and dc == 0 else away(dc)
            for dw in range(windows):
                for db in range(bands):
                    if not (first and dw == 0 and db == 0):
                        step((dc * windows + dw) * bands + db, (oc, (win + dw) % windows, (band + db) % bands))

        along(lambda dc: group(dc, False))
        group(0, True)

    def putting(off, place):
        other = (place[0] * windows + place[1]) * bands + place[2]
        return pltpu.make_async_remote_copy(
            src_ref=part_ref.at[other], dst_ref=exch_ref.at[off],
            send_sem=put_sem.at[off], recv_sem=get_sem.at[off],
            device_id=place, device_id_type=mesh_id,
        )

    pl.semaphore_wait(ready_sem, blocks - 1)
    peers(lambda off, place: putting(off, place).start())
    exch_ref[0] = part_ref[me]
    for w in range(wins):
        for h in range(RADIX // 2):
            along(lambda off: sending(off, w, h).wait_send())
    peers(lambda off, place: putting(off, place).wait_send())
    peers(lambda off, place: putting(off, place).wait_recv())
    total = jnp.sum(exch_ref[...], axis=0) * scale
    for j in range(share):
        for c in range(pieces):
            out_ref[j:j + 1, c * 128:(c + 1) * 128] = total[j * pieces + c:j * pieces + c + 1]


def body(traces, send_rows, pair_source, pair_slot, pair_owner, pair_bin, *, tables):
    sizes = tuple(lax.axis_size(name) for name in ("chan", "win", "band"))
    blocks, windows, bands = sizes
    count = math.prod(sizes)
    wins, chans, _ = traces.shape
    slot_count = send_rows.shape[2]
    slots, stacks, pairs = blocks * slot_count, blocks * BINS, pair_source.shape[0]
    share = stacks // count
    tile = (count, share * LAGS // 128, 128)
    scale = 1.0 / math.sqrt(wins * windows * NF * PAIRS_DEV / BINS)
    dma, vmem, here = pltpu.SemaphoreType.DMA, pltpu.VMEM, pl.BlockSpec(memory_space=pltpu.VMEM)
    return pl.pallas_call(
        functools.partial(kernel, sizes=sizes, scale=scale),
        out_shape=pltpu.VMEM((share, LAGS), F32),
        in_specs=[pl.BlockSpec(memory_space=pltpu.HBM)] * 8,
        out_specs=here,
        scratch_shapes=[
            vmem(send_rows.shape, jnp.int32),
            *[vmem((1, pairs), jnp.int32)] * 4,
            vmem((wins * chans, NS), BF),
            vmem((RADIX, 2, 2 * FB, LAGS), BF),
            vmem((RADIX, NQ, 2 * FB), BF),
            vmem((wins, RADIX, chans, NQ), BF),
            vmem((wins, RADIX, slots, NQ), BF),
            vmem((slots, chans), BF),
            vmem((pairs, chans), BF),
            vmem((pairs, slots), BF),
            vmem((stacks, pairs), BF),
            vmem((wins, RADIX, pairs, 2 * FB), F32),
            vmem((RADIX, pairs, 2 * FB), F32),
            vmem((blocks, wins, RADIX, slot_count, 2 * FB), BF),
            vmem((blocks, wins, RADIX, slot_count, 2 * FB), BF),
            vmem((stacks, LAGS), F32),
            vmem(tile, F32),
            vmem(tile, F32),
            dma((5,)), dma((wins * NS // KX,)), dma((2 + RADIX,)), dma((blocks, 2 * wins)), dma((blocks, 2 * wins)), dma((count,)), dma((count,)),
            pltpu.SemaphoreType.REGULAR,
        ],
        compiler_params=pltpu.CompilerParams(vmem_limit_bytes=60 << 20, collective_id=0, has_side_effects=True),
    )(
        send_rows, pair_source.reshape(1, pairs), pair_slot.reshape(1, pairs), pair_owner.reshape(1, pairs),
        pair_bin.reshape(1, pairs), traces.reshape(wins * chans, NS), *tables,
    )


def solution(mesh):
    tables = constants()
    return jax.shard_map(
        functools.partial(body, tables=tables),
        mesh=mesh,
        in_specs=(
            P("win", "chan", None),
            P("chan", None, None),
            P("chan"),
            P("chan"),
            P("chan", None),
            P("chan"),
        ),
        out_specs=P(("chan", "win", "band"), None),
        check_vma=False,
    )
```

```python
import functools
import math

import jax
import jax.numpy as jnp
import numpy as np
from jax import lax
from jax.experimental import pallas as pl
from jax.experimental.pallas import tpu as pltpu
from jax.sharding import PartitionSpec as P

NS = 4096
NF = 1024
GROUP = 32
PAIRS_DEV = 1024
BINS = 16
LAGS = 512
FLO = 128
FB = 128
RADIX = 4
NQ = NS // RADIX
KX = 512
BF = jnp.bfloat16
F32 = jnp.float32


def dot(a, b):
    return jnp.dot(a, b, preferred_element_type=F32)


def constants():
    angle = np.arange(NS, dtype=np.float64) * (2.0 * math.pi / NS)
    wave = np.stack([np.cos(angle), -np.sin(angle)]).astype(np.float32)
    freq = (FLO + np.arange(NF, dtype=np.int64)).reshape(-1, FB, RADIX).swapaxes(1, 2).reshape(-1, 1, FB)
    steps = np.arange(NQ, dtype=np.int64)[None, :, None] * freq % NS
    steps = np.concatenate([wave[0][steps], wave[1][steps]], axis=2).astype(BF)
    lag = ((np.arange(LAGS, dtype=np.int64) - LAGS // 2) % NS)[None, :]
    swap = lambda t: np.ascontiguousarray(np.swapaxes(wave[:, t], 0, 1))
    turns = swap(freq.reshape(-1, FB, 1) * lag % NS).reshape(-1, 2 * FB, LAGS)
    high = turns.astype(BF)
    low = (turns - high.astype(np.float32)).astype(BF)
    return steps, np.stack([high, low], axis=1)


def turn(ca, sa, cb, sb):
    return ca * cb - sa * sb, sa * cb + ca * sb


def split(value):
    high = value.astype(BF)
    return high, (value - high.astype(F32)).astype(BF)


def columns(row, width):
    count = row.shape[1]
    spread = jnp.transpose(jnp.broadcast_to(row.astype(F32), (128, count)))
    parts = []
    for first in range(0, width, 128):
        lane = lax.broadcasted_iota(jnp.int32, (count, 128), 1).astype(F32) + float(first)
        parts.append(jnp.where(spread == lane, 1.0, 0.0).astype(BF))
    whole = parts[0] if len(parts) == 1 else jnp.concatenate(parts, axis=1)
    return whole[:, :width]


def kernel(
    send_hbm, source_hbm, slot_hbm, owner_hbm, bin_hbm, x_hbm, steps_hbm, turns_hbm, out_ref,
    send_ref, source_ref, slot_ref, owner_ref, bin_ref, x_ref, turns_ref, table_ref, fold_ref, pick_ref, hot_ref, sh_ref, rh_ref, kh_ref,
    src_ref, cross_ref, going_ref, recv_ref, lag_ref, part_ref, exch_ref,
    list_sem, x_sem, table_sem, send_sem, recv_sem, put_sem, get_sem, ready_sem, *, sizes, scale,
):
    blocks, windows, bands = sizes
    count = blocks * windows * bands
    chan, win, band = lax.axis_index("chan"), lax.axis_index("win"), lax.axis_index("band")
    me = (chan * windows + win) * bands + band
    wins, chans = fold_ref.shape[0], fold_ref.shape[2]
    slots, slot_count = hot_ref.shape[0], going_ref.shape[3]
    pairs = sh_ref.shape[0]
    mesh_id = pl.DeviceIdType.MESH
    chunks = NQ // KX

    mine = pl.ds(band * RADIX, RADIX)
    steps = [
        pltpu.make_async_copy(steps_hbm.at[band * RADIX + j], table_ref.at[j], table_sem.at[2 + j]) for j in range(RADIX)
    ]
    lists = [
        pltpu.make_async_copy(here, there, list_sem.at[n]) for n, (here, there) in enumerate((
            (send_hbm, send_ref), (source_hbm, source_ref), (slot_hbm, slot_ref), (owner_hbm, owner_ref), (bin_hbm, bin_ref),
        ))
    ]
    later = pltpu.make_async_copy(turns_hbm.at[mine], turns_ref, table_sem.at[1])
    frames = {}
    for w in range(wins):
        for q in range(chunks):
            for a in range(RADIX):
                rows, part = pl.ds(w * chans, chans), pl.ds(a * NQ + q * KX, KX)
                frames[w, q, a] = pltpu.make_async_copy(
                    x_hbm.at[rows, part], x_ref.at[rows, part], x_sem.at[(w * chunks + q) * RADIX + a]
                )
    def fetch(w):
        for q in range(chunks):
            for a in range(RADIX):
                frames[w, q, a].start()

    for load in lists:
        load.start()
    fetch(0)
    for load in steps:
        load.start()

    barrier = pltpu.get_barrier_semaphore()

    def away(off, back=False):
        if blocks == 4:
            return {1: chan + 1 - 2 * (chan % 2), 2: (chan + 2) % 4, 3: 3 - chan}[off]
        return (chan - off + blocks) % blocks if back else (chan + off) % blocks

    def along(step):
        if blocks <= 8:
            for off in (2, 3, 1) if blocks == 4 else range(1, blocks):
                step(off)
        else:
            lax.fori_loop(1, blocks, lambda off, carry: (step(off), carry)[1], 0)

    plane = [
        (dw, db, (chan, (win + dw) % windows, (band + db) % bands))
        for dw in range(windows) for db in range(bands) if dw or db
    ]

    def hail(place, semaphore):
        pl.semaphore_signal(semaphore, inc=1, device_id=place, device_id_type=mesh_id)

    along(lambda off: hail((away(off), win, band), barrier))
    for _, _, place in plane:
        hail(place, barrier)


    for load in lists:
        load.wait()
    for w in range(1, wins):
        fetch(w)
    pick = lax.broadcasted_iota(jnp.int32, (slots, blocks), 0) // slot_count
    pick = jnp.where(pick == lax.broadcasted_iota(jnp.int32, (slots, blocks), 1), 1.0, 0.0).astype(BF)
    listed = dot(pick, send_ref[0].astype(F32).astype(BF))
    own = lax.broadcasted_iota(jnp.int32, listed.shape, 0) % slot_count
    own = own == lax.broadcasted_iota(jnp.int32, listed.shape, 1)
    listed = jnp.sum(jnp.where(own, listed, 0.0), axis=1, keepdims=True)
    lane = lax.broadcasted_iota(jnp.int32, hot_ref.shape, 1).astype(F32)
    hot_ref[...] = jnp.where(listed == lane, 1.0, 0.0).astype(BF)
    share = kh_ref.shape[0] // count
    a = lax.broadcasted_iota(jnp.int32, (2 * FB, FB), 0) % FB // (GROUP // RADIX)
    b = lax.broadcasted_iota(jnp.int32, (2 * FB, FB), 1) // (GROUP // RADIX)
    ones = jnp.where(a == b, 1.0 / GROUP, 0.0).astype(BF)

    def places():
        sh_ref[...] = columns(source_ref[...], sh_ref.shape[1])
        rh_ref[...] = columns(slot_ref[...], slots)
        row = lax.broadcasted_iota(jnp.int32, kh_ref.shape, 0)
        key = owner_ref[...] * BINS + bin_ref[...]
        kh_ref[...] = jnp.where(row % count * share + row // count == key, 1.0, 0.0).astype(BF)

    def spectra(ref, w):
        rows = ref.shape[2]
        ends = ref[w, 2:4].reshape(2 * rows, NQ)
        s0, s2 = dot(ref[w, 0], table_ref[0]), dot(ref[w, 1], table_ref[2])
        o1, o3 = dot(ends, table_ref[1]), dot(ends, table_ref[3])
        re = [s0[:, :FB], o1[:rows, :FB] + o1[rows:, FB:], s2[:, :FB], o3[:rows, :FB] - o3[rows:, FB:]]
        im = [s0[:, FB:], o1[:rows, FB:] - o1[rows:, :FB], s2[:, FB:], o3[:rows, FB:] + o3[rows:, :FB]]
        power = sum(u * u + v * v for u, v in zip(re, im))
        gain = lax.rsqrt(dot(jnp.concatenate(split(power), axis=1), ones) + 1e-05)
        return [jnp.concatenate([(u * gain).astype(BF), (v * gain).astype(BF)], axis=1) for u, v in zip(re, im)]

    def sending(off, w, h):
        other = away(off)
        part = pl.ds(0, RADIX)
        return pltpu.make_async_remote_copy(
            src_ref=going_ref.at[other, w, part], dst_ref=recv_ref.at[chan, w, part],
            send_sem=send_sem.at[off, w], recv_sem=recv_sem.at[off, w],
            device_id=(other, win, band), device_id_type=mesh_id,
        )

    def arriving(off, w, h):
        other = away(off, True)
        part = pl.ds(0, RADIX)
        return pltpu.make_async_remote_copy(
            src_ref=going_ref.at[other, w, part], dst_ref=recv_ref.at[other, w, part],
            send_sem=send_sem.at[off, w], recv_sem=recv_sem.at[off, w],
            device_id=(other, win, band), device_id_type=mesh_id,
        )

    for w in range(wins):
        rows = slice(w * chans, (w + 1) * chans)
        for q in range(chunks):
            for a in range(RADIX):
                frames[w, q, a].wait()
        if w == 0:
            for load in steps:
                load.wait()
        for q in range(chunks):
            x0, x1, x2, x3 = (x_ref[rows, a * NQ + q * KX:a * NQ + (q + 1) * KX] for a in range(RADIX))
            ends = x0 - x2, x1 - x3
            even, odd = x0.astype(F32) + x2.astype(F32), x1.astype(F32) + x3.astype(F32)
            for kind, value in enumerate(((even + odd).astype(BF), (even - odd).astype(BF), *ends)):
                fold_ref[w, kind, :, q * KX:(q + 1) * KX] = value
        for kind in range(RADIX):
            pick_ref[w, kind] = dot(hot_ref[...], fold_ref[w, kind]).astype(BF)
        for j, part in enumerate(spectra(pick_ref, w)):
            going_ref[:, w, j] = part.reshape(blocks, slot_count, 2 * FB)
        if w == 0:
            later.start()
            pl.semaphore_wait(barrier, blocks - 1 + len(plane))
            along(lambda off: hail((away(off), win, band), ready_sem))
        for h in range(1):
            along(lambda off: sending(off, w, h).start())
        recv_ref[chan, w] = going_ref[chan, w]

    places()
    for w in range(wins):
        for j, part in enumerate(spectra(fold_ref, w)):
            src_ref[w, j] = dot(sh_ref[...], part)
    later.wait()
    lag = None
    for w in range(wins):
        for j in range(RADIX):
            if j == 0:
                along(lambda off: arriving(off, w, 0).wait_recv())
            s = src_ref[w, j]
            r = dot(rh_ref[...], recv_ref[:, w, j].reshape(slots, 2 * FB))
            sre, sim, rre, rim = s[:, :FB], s[:, FB:], r[:, :FB], r[:, FB:]
            total = jnp.concatenate([sre * rre + sim * rim, sim * rre - sre * rim], axis=1)
            if w:
                total = total + cross_ref[j]
            if w < wins - 1:
                cross_ref[j] = total
                continue
            high, low = split(dot(kh_ref[...], total.astype(BF)))
            both = dot(jnp.concatenate([high, low], axis=0), turns_ref[j, 0])
            term = both[:high.shape[0]] + both[high.shape[0]:] + dot(high, turns_ref[j, 1])
            lag = term if lag is None else lag + term
    lag_ref[...] = lag

    pieces = LAGS // 128
    for j in range(share):
        for c in range(pieces):
            part_ref[:, j * pieces + c, :] = lag_ref[j * count:(j + 1) * count, c * 128:(c + 1) * 128].astype(BF)

    def peers(step):
        def group(dc, first):
            oc = (chan + dc) % blocks if isinstance(dc, int) and dc == 0 else away(dc)
            for dw in range(windows):
                for db in range(bands):
                    if not (first and dw == 0 and db == 0):
                        step((dc * windows + dw) * bands + db, (oc, (win + dw) % windows, (band + db) % bands))

        along(lambda dc: group(dc, False))
        group(0, True)

    def putting(off, place):
        other = (place[0] * windows + place[1]) * bands + place[2]
        return pltpu.make_async_remote_copy(
            src_ref=part_ref.at[other], dst_ref=exch_ref.at[off],
            send_sem=put_sem.at[off], recv_sem=get_sem.at[off],
            device_id=place, device_id_type=mesh_id,
        )

    pl.semaphore_wait(ready_sem, blocks - 1)
    peers(lambda off, place: putting(off, place).start())
    exch_ref[0] = part_ref[me]
    for w in range(wins):
        for h in range(1):
            along(lambda off: sending(off, w, h).wait_send())
    peers(lambda off, place: putting(off, place).wait_send())
    peers(lambda off, place: putting(off, place).wait_recv())
    total = jnp.sum(exch_ref[...].astype(F32), axis=0) * scale
    for j in range(share):
        for c in range(pieces):
            out_ref[j:j + 1, c * 128:(c + 1) * 128] = total[j * pieces + c:j * pieces + c + 1]


def body(traces, send_rows, pair_source, pair_slot, pair_owner, pair_bin, *, tables):
    sizes = tuple(lax.axis_size(name) for name in ("chan", "win", "band"))
    blocks, windows, bands = sizes
    count = math.prod(sizes)
    wins, chans, _ = traces.shape
    slot_count = send_rows.shape[2]
    slots, stacks, pairs = blocks * slot_count, blocks * BINS, pair_source.shape[0]
    share = stacks // count
    tile = (count, share * LAGS // 128, 128)
    scale = 1.0 / math.sqrt(wins * windows * NF * PAIRS_DEV / BINS)
    dma, vmem, here = pltpu.SemaphoreType.DMA, pltpu.VMEM, pl.BlockSpec(memory_space=pltpu.VMEM)
    return pl.pallas_call(
        functools.partial(kernel, sizes=sizes, scale=scale),
        out_shape=pltpu.VMEM((share, LAGS), F32),
        in_specs=[pl.BlockSpec(memory_space=pltpu.HBM)] * 8,
        out_specs=here,
        scratch_shapes=[
            vmem(send_rows.shape, jnp.int32),
            *[vmem((1, pairs), jnp.int32)] * 4,
            vmem((wins * chans, NS), BF),
            vmem((RADIX, 2, 2 * FB, LAGS), BF),
            vmem((RADIX, NQ, 2 * FB), BF),
            vmem((wins, RADIX, chans, NQ), BF),
            vmem((wins, RADIX, slots, NQ), BF),
            vmem((slots, chans), BF),
            vmem((pairs, chans), BF),
            vmem((pairs, slots), BF),
            vmem((stacks, pairs), BF),
            vmem((wins, RADIX, pairs, 2 * FB), F32),
            vmem((RADIX, pairs, 2 * FB), F32),
            vmem((blocks, wins, RADIX, slot_count, 2 * FB), BF),
            vmem((blocks, wins, RADIX, slot_count, 2 * FB), BF),
            vmem((stacks, LAGS), F32),
            vmem(tile, BF),
            vmem(tile, BF),
            dma((5,)), dma((wins * NS // KX,)), dma((2 + RADIX,)), dma((blocks, wins)), dma((blocks, wins)), dma((count,)), dma((count,)),
            pltpu.SemaphoreType.REGULAR,
        ],
        compiler_params=pltpu.CompilerParams(vmem_limit_bytes=60 << 20, collective_id=0, has_side_effects=True),
    )(
        send_rows, pair_source.reshape(1, pairs), pair_slot.reshape(1, pairs), pair_owner.reshape(1, pairs),
        pair_bin.reshape(1, pairs), traces.reshape(wins * chans, NS), *tables,
    )


def solution(mesh):
    tables = constants()
    return jax.shard_map(
        functools.partial(body, tables=tables),
        mesh=mesh,
        in_specs=(
            P("win", "chan", None),
            P("chan", None, None),
            P("chan"),
            P("chan"),
            P("chan", None),
            P("chan"),
        ),
        out_specs=P(("chan", "win", "band"), None),
        check_vma=False,
    )
```
